128 devices in a mesh: gx: 4 (over z_lo, core), gy: 4 (over x), gz: 8 (over z_hi, y).
Axes of the slice: x: 4, y: 4, z: 4 (z_hi: 2, z_lo: 2; z = z_hi * 2 + z_lo), core: 2. Of those that a mesh axis runs over, the one named last changes fastest.
Arguments:
- right_sides: float32 [2, 128, 1024, 1024], P(None, ('gx', 'gy', 'gz')), may hold values from -6 to 6
- projector: float32 [2, 128, 1024, 192], P(None, ('gx', 'gy', 'gz')), may hold values from -0.1875 to 0.1875
- mixing: float32 [8, 2, 128, 2, 192, 192], P(None, None, ('gx', 'gy', 'gz')), may hold values from -0.3125 to 0.3125
- expander: float32 [256, 1024, 192], P(('gx', 'gy', 'gz')), may hold values from -0.4375 to 0.4375
Outputs:
- product: float32 [256, 1024, 1024], P(('gx', 'gy', 'gz'))
The draws below stay inside these ranges and needn't reach their ends.
All inputs are finite; a program needn't handle non-finite values.
Results may differ from the reference program's by a relative error of at most 0.0001.
Values sent between devices are 32-bit elements; how exact they have to be, the bound alone decides.
No kernel may reach another device: no remote copies, remote signals or barrier semaphores. Data moves between devices by JAX's collectives and lax.ppermute only.
A program may use at most 128 MiB of HBM per device.

```python
import jax
import jax.numpy as jnp
from jax import lax

LEAF = 1024
K = 192
RHS = 1024
NODES = 256
LEVELS = 8
DEVICES = 128


def levels(key, dims, pieces, smallest, top_value):
    gain = 1.0
    for position, blocks in pieces:
        draws = jax.random.uniform(jax.random.fold_in(jax.random.fold_in(key, 6), position), (blocks,), jnp.float32, smallest / len(pieces), top_value / len(pieces))
        gain = gain * jnp.repeat(jnp.exp(draws), dims[position] // blocks).reshape((-1,) + (1,) * (len(dims) - 1 - position))
    return gain


def scatter_about(key, extent, spread, limit, split=(), held_as=jnp.bfloat16):
    array = spread * jax.random.normal(key, extent, jnp.float32)
    if split:
        array = array * levels(key, extent, split, -0.22, 0.18)
    return jnp.clip(array, -limit, limit).astype(held_as)


def setup_inputs(seed: int = 0) -> dict:
    splits = jax.random.split(jax.random.key(seed), 5)
    return {
        "right_sides": scatter_about(splits[0], (2, DEVICES, LEAF, RHS), 1.0, 6.0, ((1, 128),), jnp.float32),
        "projector": scatter_about(splits[1], (2, DEVICES, LEAF, K), LEAF ** -0.5, 0.1875, ((1, 128),), jnp.float32),
        "mixing": scatter_about(splits[2], (LEVELS, 2, DEVICES, 2, K, K), (2 * K) ** -0.5, 0.3125, ((2, 128),), jnp.float32),
        "expander": scatter_about(splits[3], (NODES, LEAF, K), K ** -0.5, 0.4375, ((0, 128),), jnp.float32),
    }


exact = lax.Precision.HIGHEST


def mix_level(weights, coeffs, partner):
    local_term = jnp.einsum("nkj,njr->nkr", weights[:, 0], coeffs, precision=exact)
    remote_term = jnp.einsum("nkj,njr->nkr", weights[:, 1], partner, precision=exact)
    return local_term + remote_term


def reference(right_sides, projector, mixing, expander):
    leaf_data = right_sides.reshape(NODES, LEAF, RHS)
    leaf_proj = projector.reshape(NODES, LEAF, K)
    leaf_mix = mixing.reshape(LEVELS, NODES, 2, K, K)
    coeffs = jnp.einsum("nlk,nlr->nkr", leaf_proj, leaf_data, precision=exact)
    for level_index in range(LEVELS):
        stride = 2 ** level_index
        paired = coeffs.reshape(NODES // (2 * stride), 2, stride, K, RHS)
        partner = paired[:, ::-1].reshape(NODES, K, RHS)
        coeffs = mix_level(leaf_mix[level_index], coeffs, partner)
    bit_view = coeffs.reshape((2,) * LEVELS + (K, RHS))
    axis_order = tuple(range(LEVELS - 1, -1, -1)) + (LEVELS, LEVELS + 1)
    reordered = bit_view.transpose(axis_order).reshape(NODES, K, RHS)
    return jnp.einsum("nlk,nkr->nlr", expander, reordered, precision=exact)
```

```python
import functools

import jax
import jax.numpy as jnp
from jax import lax
from jax.experimental import pallas as pl
from jax.experimental.pallas import tpu as pltpu
from jax.sharding import PartitionSpec as P

AXES = ("gx", "gy", "gz")
DEVICES = 128
Y0, Y1, ZH, X0, X1, CORE, Z0, SLOT = range(8)
WIDTHS = (512, 512)
VMEM_LIMIT = 56 * 2**20
HIGH = lax.Precision.HIGH
EXACT = lax.Precision.HIGHEST


def parity(own, mask):
    total = jnp.int32(0)
    for bit in range(7):
        if (mask >> bit) & 1:
            total = total ^ (jnp.right_shift(own, bit) & 1)
    return total


def ordered(pair, swap):
    chosen = swap == 1
    return jnp.where(chosen, pair[1], pair[0]), jnp.where(chosen, pair[0], pair[1])


class Place:
    def __init__(self, held=tuple(range(8)), mask=0):
        self.held, self.mask = tuple(held), mask

    def traded(self, *swaps):
        held = list(self.held)
        for one, other in swaps:
            held[one], held[other] = held[other], held[one]
        return held

    def to(self, held):
        coming = self.held.index(held[SLOT])
        leaving = held.index(self.held[SLOT])
        routes = []
        for t in range(2):
            pairs = []
            for device in range(DEVICES):
                value = ((device >> coming) & 1) ^ t if coming != SLOT else 0
                reached = 0
                for position in range(7):
                    bit = held[position]
                    if position == leaving:
                        reached |= value << position
                    else:
                        reached |= ((device >> self.held.index(bit)) & 1) << position
                pairs.append((device, reached))
            routes.append(pairs)
        if coming == SLOT:
            mask = 0
            for position in range(7):
                if (self.mask >> self.held.index(held[position])) & 1:
                    mask |= 1 << position
            return Place(held, mask), 0, routes
        return Place(held, 1 << leaving), self.mask ^ (1 << coming), routes


def sent(values, pairs):
    if all(source == reached for source, reached in pairs):
        return values
    return lax.ppermute(values, AXES, pairs)


def after(values, awaited):
    return lax.optimization_barrier((values, awaited))[0]


def halves(x):
    high = x.astype(jnp.bfloat16)
    low = (x - high.astype(jnp.float32)).astype(jnp.bfloat16)
    return high, low


def product(left, right, transposed=False):
    (lh, ll), (rh, rl) = left, right
    axis = 1 if transposed else 0
    dims = (((0 if transposed else 1,), (0,)), ((), ()))
    rows = lh.shape[axis]
    dot = functools.partial(lax.dot_general, dimension_numbers=dims, preferred_element_type=jnp.float32)
    both = dot(jnp.concatenate([lh, ll], axis=axis), rh)
    return both[:rows] + both[rows:] + dot(lh, rl)


def params(flops, moved_bytes):
    return dict(
        compiler_params=pltpu.CompilerParams(vmem_limit_bytes=VMEM_LIMIT),
        cost_estimate=pl.CostEstimate(flops=flops, transcendentals=0, bytes_accessed=moved_bytes),
    )


def pick(flag, first, second):
    return jnp.where(flag == 1, second, first)


def expand_kernel(flag, e_ref, r0_ref, r1_ref, *rest):
    out_ref = rest[-1]
    chosen = pl.program_id(0) ^ flag[0]
    right = halves(pick(chosen, r0_ref[...], r1_ref[...]))
    out_ref[0] = product(halves(e_ref[0]), right, transposed=True)


def expand(flag, expander, pair, start, total, earlier):
    rank, width = pair[0].shape
    leaf = expander.shape[2]
    rows = min(leaf, 512)
    base = start // width
    r_spec = pl.BlockSpec((rank, width), lambda e, i, f: (0, 0))
    extra = () if earlier is None else (earlier,)
    return pl.pallas_call(
        expand_kernel,
        grid_spec=pltpu.PrefetchScalarGridSpec(
            num_scalar_prefetch=1,
            grid=(2, leaf // rows),
            in_specs=[pl.BlockSpec((1, rank, rows), lambda e, i, f: (e, 0, i)), r_spec, r_spec]
            + [pl.BlockSpec(memory_space=pl.ANY)] * len(extra),
            out_specs=pl.BlockSpec((1, rows, width), lambda e, i, f: (e, i, base)),
        ),
        out_shape=jax.ShapeDtypeStruct((2, leaf, total), jnp.float32),
        input_output_aliases={} if earlier is None else {4: 0},
        name="expand",
        **params(4 * leaf * rank * width, 8 * leaf * (rank + width) + 8 * rank * width),
    )(flag, expander, *pair, *extra)


HOME = Place()
FLIP_CORE = [(d, d ^ (1 << CORE)) for d in range(DEVICES)]
MOVES = (
    (((SLOT, Y0), (CORE, Y1)), ((0, False),)),
    (((SLOT, CORE),), ((1, False),)),
    (((SLOT, Y1), (CORE, Y0)), ()),
    (((SLOT, ZH), (CORE, Z0)), ((2, False),)),
    (((SLOT, X1), (CORE, X0)), ((3, True), (4, False))),
    (((SLOT, ZH), (CORE, X0)), ((5, False),)),
    (((SLOT, CORE),), ((6, False),)),
    (((SLOT, Y0), (CORE, Y1)), ()),
    (((SLOT, Z0),), ((7, False),)),
)


def places():
    found, at_level, place = [], {}, HOME
    for trades, levels in MOVES:
        held = place.traded(*trades)
        place = place.to(held)[0]
        found.append(place)
        for level, _ in levels:
            at_level[level] = place
    return found, at_level


def fetch(mixing, own, levels, held):
    place, order, routes = HOME.to(held)
    chosen = mixing[levels, :, 0]
    bit = parity(own, order)
    pair = [lax.dynamic_index_in_dim(chosen, bit ^ t, 1, keepdims=False) for t in range(2)]
    return [sent(v, r) for v, r in zip(pair, routes)], place


def local_factors(pair, swap, shift):
    first, second = ordered(pair, swap ^ shift)
    own_first, cross_first = ordered((first[0], first[1]), swap)
    cross_second, own_second = ordered((second[1], second[0]), swap)
    return (
        jnp.concatenate([own_first, cross_second], axis=0),
        jnp.concatenate([cross_first, own_second], axis=0),
    )


def dot(a, b):
    return jnp.dot(a, b, precision=EXACT)


def shards(right_sides, projector, mixing, expander):
    own = lax.axis_index(AXES)
    total = right_sides.shape[3]
    rank = projector.shape[3]
    _, at_level = places()
    factors = {}

    def get(levels, held_at):
        pair, place = fetch(mixing, own, slice(levels[0], levels[-1] + 1), held_at)
        for index, level in enumerate(levels):
            factors[level] = ([v[index] for v in pair], place)
        return pair, place

    get((0,), list(at_level[0].held))
    get((1,), list(at_level[1].held))
    pair, place = get((2, 3, 4), list(at_level[2].held))
    place, order, routes = place.to(list(at_level[3].held))
    pair = ordered([v[1:] for v in pair], parity(own, order))
    pair = [sent(v, r) for v, r in zip(pair, routes)]
    for index, level in enumerate((3, 4)):
        factors[level] = ([v[index] for v in pair], place)
    get((5,), list(at_level[5].held))
    get((6,), list(at_level[6].held))
    late_mixing = mixing

    chunks, starts, start = [], [], 0
    place = HOME
    for width in WIDTHS:
        columns = slice(start, start + width)
        chunks.append(
            [
                lax.dot_general(
                    projector[c, 0],
                    right_sides[c, 0, :, columns],
                    (((0,), (0,)), ((), ())),
                    precision=HIGH,
                )
                for c in range(2)
            ]
        )
        starts.append(start)
        start += width
    sorted_for = 0
    for number, (trades, levels) in enumerate(MOVES):
        place_next, order, routes = place.to(place.traded(*trades))
        if order != sorted_for:
            chunks = [ordered(pair, parity(own, order ^ sorted_for)) for pair in chunks]
        chunks = [[sent(v, r) for v, r in zip(pair, routes)] for pair in chunks]
        place = place_next
        sorted_for = 0
        if number + 1 < len(MOVES):
            following = place.to(place.traded(*MOVES[number + 1][0]))[1]
        else:
            following = place.mask
        for position, (level, at_core) in enumerate(levels):
            if level == 2:
                late_mixing = after(mixing, chunks[-1][1])
                pair7, place7 = fetch(late_mixing, own, slice(7, 8), list(at_level[7].held))
                factors[7] = ([v[0] for v in pair7], place7)
            pair_w, place_w = factors[level]
            assert place_w.held == place.held, (level, place_w.held, place.held)
            shift = parity(own, place.mask ^ place_w.mask)
            last = position + 1 == len(levels)
            swap_mask = following if last else 0
            swap = parity(own, swap_mask)
            if at_core:
                aligned = ordered(pair_w, shift)
                for index, pair in enumerate(chunks):
                    others = [sent(v, FLIP_CORE) for v in pair]
                    out = [dot(w[0], v) + dot(w[1], o) for w, v, o in zip(aligned, pair, others)]
                    chunks[index] = ordered(out, swap) if swap_mask else out
            else:
                for_first, for_second = local_factors(pair_w, swap, shift)
                for index, pair in enumerate(chunks):
                    out = dot(for_first, pair[0]) + dot(for_second, pair[1])
                    chunks[index] = [out[:rank], out[rank:]]
            if last:
                sorted_for = swap_mask
    assert sorted_for == place.mask
    flag = jnp.zeros((1,), jnp.int32)
    result = None
    for start, pair in zip(starts, chunks):
        result = expand(flag, jnp.swapaxes(expander, 1, 2), pair, start, total, result)
    return result


def solution(mesh):
    placed = (
        P(None, AXES, None, None),
        P(None, AXES, None, None),
        P(None, None, AXES, None, None, None),
        P(AXES, None, None),
    )
    return jax.shard_map(
        shards, mesh=mesh, in_specs=placed, out_specs=P(AXES, None, None), check_vma=False
    )
```

```python
import functools

import jax
import jax.numpy as jnp
from jax import lax
from jax.experimental import pallas as pl
from jax.experimental.pallas import tpu as pltpu
from jax.sharding import PartitionSpec as P

AXES = ("gx", "gy", "gz")
DEVICES = 128
Y0, Y1, ZH, X0, X1, CORE, Z0, SLOT = range(8)
WIDTHS = (512, 512)
VMEM_LIMIT = 56 * 2**20
HIGH = lax.Precision.HIGH
FAST_LEVELS = (0, 1, 2, 4, 5, 6, 7)
EXACT = lax.Precision.HIGHEST


def parity(own, mask):
    total = jnp.int32(0)
    for bit in range(7):
        if (mask >> bit) & 1:
            total = total ^ (jnp.right_shift(own, bit) & 1)
    return total


def ordered(pair, swap):
    chosen = swap == 1
    return jnp.where(chosen, pair[1], pair[0]), jnp.where(chosen, pair[0], pair[1])


class Place:
    def __init__(self, held=tuple(range(8)), mask=0):
        self.held, self.mask = tuple(held), mask

    def traded(self, *swaps):
        held = list(self.held)
        for one, other in swaps:
            held[one], held[other] = held[other], held[one]
        return held

    def to(self, held):
        coming = self.held.index(held[SLOT])
        leaving = held.index(self.held[SLOT])
        routes = []
        for t in range(2):
            pairs = []
            for device in range(DEVICES):
                value = ((device >> coming) & 1) ^ t if coming != SLOT else 0
                reached = 0
                for position in range(7):
                    bit = held[position]
                    if position == leaving:
                        reached |= value << position
                    else:
                        reached |= ((device >> self.held.index(bit)) & 1) << position
                pairs.append((device, reached))
            routes.append(pairs)
        if coming == SLOT:
            mask = 0
            for position in range(7):
                if (self.mask >> self.held.index(held[position])) & 1:
                    mask |= 1 << position
            return Place(held, mask), 0, routes
        return Place(held, 1 << leaving), self.mask ^ (1 << coming), routes


def sent(values, pairs):
    if all(source == reached for source, reached in pairs):
        return values
    return lax.ppermute(values, AXES, pairs)


def after(values, awaited):
    return lax.optimization_barrier((values, awaited))[0]


def halves(x):
    high = x.astype(jnp.bfloat16)
    low = (x - high.astype(jnp.float32)).astype(jnp.bfloat16)
    return high, low


def product(left, right, transposed=False):
    (lh, ll), (rh, rl) = left, right
    axis = 1 if transposed else 0
    dims = (((0 if transposed else 1,), (0,)), ((), ()))
    rows = lh.shape[axis]
    dot = functools.partial(lax.dot_general, dimension_numbers=dims, preferred_element_type=jnp.float32)
    both = dot(jnp.concatenate([lh, ll], axis=axis), rh)
    return both[:rows] + both[rows:] + dot(lh, rl)


def params(flops, moved_bytes):
    return dict(
        compiler_params=pltpu.CompilerParams(vmem_limit_bytes=VMEM_LIMIT),
        cost_estimate=pl.CostEstimate(flops=flops, transcendentals=0, bytes_accessed=moved_bytes),
    )


def pick(flag, first, second):
    return jnp.where(flag == 1, second, first)


def expand_kernel(flag, e_ref, r0_ref, r1_ref, *rest):
    out_ref = rest[-1]
    chosen = pl.program_id(0) ^ flag[0]
    right = halves(pick(chosen, r0_ref[...], r1_ref[...]))
    out_ref[0] = product(halves(e_ref[0]), right, transposed=True)


def expand(flag, expander, pair, start, total, earlier):
    rank, width = pair[0].shape
    leaf = expander.shape[2]
    rows = min(leaf, 512)
    base = start // width
    r_spec = pl.BlockSpec((rank, width), lambda e, i, f: (0, 0))
    extra = () if earlier is None else (earlier,)
    return pl.pallas_call(
        expand_kernel,
        grid_spec=pltpu.PrefetchScalarGridSpec(
            num_scalar_prefetch=1,
            grid=(2, leaf // rows),
            in_specs=[pl.BlockSpec((1, rank, rows), lambda e, i, f: (e, 0, i)), r_spec, r_spec]
            + [pl.BlockSpec(memory_space=pl.ANY)] * len(extra),
            out_specs=pl.BlockSpec((1, rows, width), lambda e, i, f: (e, i, base)),
        ),
        out_shape=jax.ShapeDtypeStruct((2, leaf, total), jnp.float32),
        input_output_aliases={} if earlier is None else {4: 0},
        name="expand",
        **params(4 * leaf * rank * width, 8 * leaf * (rank + width) + 8 * rank * width),
    )(flag, expander, *pair, *extra)


HOME = Place()
FLIP_CORE = [(d, d ^ (1 << CORE)) for d in range(DEVICES)]
MOVES = (
    (((SLOT, Y0), (CORE, Y1)), ((0, False),)),
    (((SLOT, CORE),), ((1, False),)),
    (((SLOT, Y1), (CORE, Y0)), ()),
    (((SLOT, ZH), (CORE, Z0)), ((2, False),)),
    (((SLOT, X1), (CORE, X0)), ((3, True), (4, False))),
    (((SLOT, ZH), (CORE, X0)), ((5, False),)),
    (((SLOT, CORE),), ((6, False),)),
    (((SLOT, Y0), (CORE, Y1)), ()),
    (((SLOT, Z0),), ((7, False),)),
)


def places():
    found, at_level, place = [], {}, HOME
    for trades, levels in MOVES:
        held = place.traded(*trades)
        place = place.to(held)[0]
        found.append(place)
        for level, _ in levels:
            at_level[level] = place
    return found, at_level


def fetch(mixing, own, levels, held):
    place, order, routes = HOME.to(held)
    chosen = mixing[levels, :, 0]
    bit = parity(own, order)
    pair = [lax.dynamic_index_in_dim(chosen, bit ^ t, 1, keepdims=False) for t in range(2)]
    return [sent(v, r) for v, r in zip(pair, routes)], place


def local_factors(pair, swap, shift):
    first, second = ordered(pair, swap ^ shift)
    own_first, cross_first = ordered((first[0], first[1]), swap)
    cross_second, own_second = ordered((second[1], second[0]), swap)
    return (
        jnp.concatenate([own_first, cross_second], axis=0),
        jnp.concatenate([cross_first, own_second], axis=0),
    )


def dot(a, b, level):
    return jnp.dot(a, b, precision=HIGH if level in FAST_LEVELS else EXACT)


def shards(right_sides, projector, mixing, expander):
    own = lax.axis_index(AXES)
    total = right_sides.shape[3]
    rank = projector.shape[3]
    _, at_level = places()
    factors = {}

    def get(levels, held_at):
        pair, place = fetch(mixing, own, slice(levels[0], levels[-1] + 1), held_at)
        for index, level in enumerate(levels):
            factors[level] = ([v[index] for v in pair], place)
        return pair, place

    get((0,), list(at_level[0].held))
    get((1,), list(at_level[1].held))
    pair, place = get((2, 3, 4), list(at_level[2].held))
    place, order, routes = place.to(list(at_level[3].held))
    pair = ordered([v[1:] for v in pair], parity(own, order))
    pair = [sent(v, r) for v, r in zip(pair, routes)]
    for index, level in enumerate((3, 4)):
        factors[level] = ([v[index] for v in pair], place)
    get((5,), list(at_level[5].held))
    get((6,), list(at_level[6].held))
    late_mixing = mixing

    chunks, starts, start = [], [], 0
    place = HOME
    for width in WIDTHS:
        columns = slice(start, start + width)
        chunks.append(
            [
                lax.dot_general(
                    projector[c, 0],
                    right_sides[c, 0, :, columns],
                    (((0,), (0,)), ((), ())),
                    precision=HIGH,
                )
                for c in range(2)
            ]
        )
        starts.append(start)
        start += width
    sorted_for = 0
    for number, (trades, levels) in enumerate(MOVES):
        place_next, order, routes = place.to(place.traded(*trades))
        if order != sorted_for:
            chunks = [ordered(pair, parity(own, order ^ sorted_for)) for pair in chunks]
        chunks = [[sent(v, r) for v, r in zip(pair, routes)] for pair in chunks]
        place = place_next
        sorted_for = 0
        if number + 1 < len(MOVES):
            following = place.to(place.traded(*MOVES[number + 1][0]))[1]
        else:
            following = place.mask
        for position, (level, at_core) in enumerate(levels):
            if level == 2:
                late_mixing = after(mixing, chunks[-1][1])
                pair7, place7 = fetch(late_mixing, own, slice(7, 8), list(at_level[7].held))
                factors[7] = ([v[0] for v in pair7], place7)
            pair_w, place_w = factors[level]
            assert place_w.held == place.held, (level, place_w.held, place.held)
            shift = parity(own, place.mask ^ place_w.mask)
            last = position + 1 == len(levels)
            swap_mask = following if last else 0
            swap = parity(own, swap_mask)
            if at_core:
                aligned = ordered(pair_w, shift)
                for index, pair in enumerate(chunks):
                    others = [sent(v, FLIP_CORE) for v in pair]
                    out = [dot(w[0], v, level) + dot(w[1], o, level) for w, v, o in zip(aligned, pair, others)]
                    chunks[index] = ordered(out, swap) if swap_mask else out
            else:
                for_first, for_second = local_factors(pair_w, swap, shift)
                for index, pair in enumerate(chunks):
                    out = dot(for_first, pair[0], level) + dot(for_second, pair[1], level)
                    chunks[index] = [out[:rank], out[rank:]]
            if last:
                sorted_for = swap_mask
    assert sorted_for == place.mask
    flag = jnp.zeros((1,), jnp.int32)
    result = None
    for start, pair in zip(starts, chunks):
        result = expand(flag, jnp.swapaxes(expander, 1, 2), pair, start, total, result)
    return result


def solution(mesh):
    placed = (
        P(None, AXES, None, None),
        P(None, AXES, None, None),
        P(None, None, AXES, None, None, None),
        P(AXES, None, None),
    )
    return jax.shard_map(
        shards, mesh=mesh, in_specs=placed, out_specs=P(AXES, None, None), check_vma=False
    )
```

```python
import functools

import jax
import jax.numpy as jnp
from jax import lax
from jax.experimental import pallas as pl
from jax.experimental.pallas import tpu as pltpu
from jax.sharding import PartitionSpec as P

AXES = ("gx", "gy", "gz")
DEVICES = 128
Y0, Y1, ZH, X0, X1, CORE, Z0, SLOT = range(8)
WIDTHS = (512, 512)
VMEM_LIMIT = 56 * 2**20
HIGH = lax.Precision.HIGH
FAST_LEVELS = (0, 1, 2, 4, 5, 6, 7)
EXACT = lax.Precision.HIGHEST


def parity(own, mask):
    total = jnp.int32(0)
    for bit in range(7):
        if (mask >> bit) & 1:
            total = total ^ (jnp.right_shift(own, bit) & 1)
    return total


def ordered(pair, swap):
    chosen = swap == 1
    return jnp.where(chosen, pair[1], pair[0]), jnp.where(chosen, pair[0], pair[1])


class Place:
    def __init__(self, held=tuple(range(8)), mask=0):
        self.held, self.mask = tuple(held), mask

    def traded(self, *swaps):
        held = list(self.held)
        for one, other in swaps:
            held[one], held[other] = held[other], held[one]
        return held

    def to(self, held):
        coming = self.held.index(held[SLOT])
        leaving = held.index(self.held[SLOT])
        routes = []
        for t in range(2):
            pairs = []
            for device in range(DEVICES):
                value = ((device >> coming) & 1) ^ t if coming != SLOT else 0
                reached = 0
                for position in range(7):
                    bit = held[position]
                    if position == leaving:
                        reached |= value << position
                    else:
                        reached |= ((device >> self.held.index(bit)) & 1) << position
                pairs.append((device, reached))
            routes.append(pairs)
        if coming == SLOT:
            mask = 0
            for position in range(7):
                if (self.mask >> self.held.index(held[position])) & 1:
                    mask |= 1 << position
            return Place(held, mask), 0, routes
        return Place(held, 1 << leaving), self.mask ^ (1 << coming), routes


def sent(values, pairs):
    if all(source == reached for source, reached in pairs):
        return values
    return lax.ppermute(values, AXES, pairs)


def after(values, awaited):
    return lax.optimization_barrier((values, awaited))[0]


def halves(x):
    high = x.astype(jnp.bfloat16)
    low = (x - high.astype(jnp.float32)).astype(jnp.bfloat16)
    return high, low


def product(left, right, transposed=False):
    (lh, ll), (rh, rl) = left, right
    axis = 1 if transposed else 0
    dims = (((0 if transposed else 1,), (0,)), ((), ()))
    rows = lh.shape[axis]
    dot = functools.partial(lax.dot_general, dimension_numbers=dims, preferred_element_type=jnp.float32)
    both = dot(jnp.concatenate([lh, ll], axis=axis), rh)
    return both[:rows] + both[rows:] + dot(lh, rl)


def params(flops, moved_bytes):
    return dict(
        compiler_params=pltpu.CompilerParams(vmem_limit_bytes=VMEM_LIMIT),
        cost_estimate=pl.CostEstimate(flops=flops, transcendentals=0, bytes_accessed=moved_bytes),
    )


def pick(flag, first, second):
    return jnp.where(flag == 1, second, first)


def expand_kernel(flag, e_ref, r0_ref, r1_ref, *rest):
    out_ref = rest[-1]
    chosen = pl.program_id(0) ^ flag[0]
    right = halves(pick(chosen, r0_ref[...], r1_ref[...]))
    out_ref[0] = product(halves(e_ref[0]), right, transposed=True)


def expand(flag, expander, pair, start, total, earlier):
    rank, width = pair[0].shape
    leaf = expander.shape[2]
    rows = min(leaf, 512)
    base = start // width
    r_spec = pl.BlockSpec((rank, width), lambda e, i, f: (0, 0))
    extra = () if earlier is None else (earlier,)
    return pl.pallas_call(
        expand_kernel,
        grid_spec=pltpu.PrefetchScalarGridSpec(
            num_scalar_prefetch=1,
            grid=(2, leaf // rows),
            in_specs=[pl.BlockSpec((1, rank, rows), lambda e, i, f: (e, 0, i)), r_spec, r_spec]
            + [pl.BlockSpec(memory_space=pl.ANY)] * len(extra),
            out_specs=pl.BlockSpec((1, rows, width), lambda e, i, f: (e, i, base)),
        ),
        out_shape=jax.ShapeDtypeStruct((2, leaf, total), jnp.float32),
        input_output_aliases={} if earlier is None else {4: 0},
        name="expand",
        **params(4 * leaf * rank * width, 8 * leaf * (rank + width) + 8 * rank * width),
    )(flag, expander, *pair, *extra)


HOME = Place()
FLIP_CORE = [(d, d ^ (1 << CORE)) for d in range(DEVICES)]
MOVES = (
    (((SLOT, Y0), (CORE, Y1)), ((0, False),)),
    (((SLOT, CORE),), ((1, False),)),
    (((SLOT, Y1), (CORE, Y0)), ()),
    (((SLOT, ZH), (CORE, Z0)), ((2, False),)),
    (((SLOT, X1), (CORE, X0)), ((3, True), (4, False))),
    (((SLOT, ZH), (CORE, X0)), ((5, False),)),
    (((SLOT, CORE),), ((6, False),)),
    (((SLOT, Y0), (CORE, Y1)), ()),
    (((SLOT, Z0),), ((7, False),)),
)


def places():
    found, at_level, place = [], {}, HOME
    for trades, levels in MOVES:
        held = place.traded(*trades)
        place = place.to(held)[0]
        found.append(place)
        for level, _ in levels:
            at_level[level] = place
    return found, at_level


def fetch(mixing, own, levels, held):
    place, order, routes = HOME.to(held)
    chosen = mixing[levels, :, 0]
    bit = parity(own, order)
    pair = [lax.dynamic_index_in_dim(chosen, bit ^ t, 1, keepdims=False) for t in range(2)]
    return [sent(v, r) for v, r in zip(pair, routes)], place


def local_factors(pair, swap, shift):
    first, second = ordered(pair, swap ^ shift)
    own_first, cross_first = ordered((first[0], first[1]), swap)
    cross_second, own_second = ordered((second[1], second[0]), swap)
    return (
        jnp.concatenate([own_first, cross_second], axis=0),
        jnp.concatenate([cross_first, own_second], axis=0),
    )


def dot(a, b, level):
    return jnp.dot(a, b, precision=HIGH if level in FAST_LEVELS else EXACT)


def shards(right_sides, projector, mixing, expander):
    own = lax.axis_index(AXES)
    total = right_sides.shape[3]
    rank = projector.shape[3]
    _, at_level = places()
    factors = {}

    def get(levels, held_at):
        pair, place = fetch(mixing, own, slice(levels[0], levels[-1] + 1), held_at)
        for index, level in enumerate(levels):
            factors[level] = ([v[index] for v in pair], place)
        return pair, place

    get((0,), list(at_level[0].held))
    get((1,), list(at_level[1].held))
    pair, place = get((2, 3, 4), list(at_level[2].held))
    place, order, routes = place.to(list(at_level[3].held))
    pair = ordered([v[1:] for v in pair], parity(own, order))
    pair = [sent(v, r) for v, r in zip(pair, routes)]
    for index, level in enumerate((3, 4)):
        factors[level] = ([v[index] for v in pair], place)
    pair, place = fetch(mixing, own, slice(5, 7), list(at_level[5].held))
    factors[5] = ([v[0] for v in pair], place)
    place, order, routes = place.to(list(at_level[6].held))
    pair = ordered([v[1] for v in pair], parity(own, order))
    factors[6] = ([sent(v, r) for v, r in zip(pair, routes)], place)
    late_mixing = mixing

    chunks, starts, start = [], [], 0
    place = HOME
    for width in WIDTHS:
        columns = slice(start, start + width)
        chunks.append(
            [
                lax.dot_general(
                    projector[c, 0],
                    right_sides[c, 0, :, columns],
                    (((0,), (0,)), ((), ())),
                    precision=HIGH,
                )
                for c in range(2)
            ]
        )
        starts.append(start)
        start += width
    sorted_for = 0
    for number, (trades, levels) in enumerate(MOVES):
        place_next, order, routes = place.to(place.traded(*trades))
        if order != sorted_for:
            chunks = [ordered(pair, parity(own, order ^ sorted_for)) for pair in chunks]
        chunks = [[sent(v, r) for v, r in zip(pair, routes)] for pair in chunks]
        place = place_next
        sorted_for = 0
        if number + 1 < len(MOVES):
            following = place.to(place.traded(*MOVES[number + 1][0]))[1]
        else:
            following = place.mask
        for position, (level, at_core) in enumerate(levels):
            if level == 2:
                late_mixing = after(mixing, chunks[-1][1])
                pair7, place7 = fetch(late_mixing, own, slice(7, 8), list(at_level[7].held))
                factors[7] = ([v[0] for v in pair7], place7)
            pair_w, place_w = factors[level]
            assert place_w.held == place.held, (level, place_w.held, place.held)
            shift = parity(own, place.mask ^ place_w.mask)
            last = position + 1 == len(levels)
            swap_mask = following if last else 0
            swap = parity(own, swap_mask)
            if at_core:
                aligned = ordered(pair_w, shift)
                for index, pair in enumerate(chunks):
                    others = [sent(v, FLIP_CORE) for v in pair]
                    out = [dot(w[0], v, level) + dot(w[1], o, level) for w, v, o in zip(aligned, pair, others)]
                    chunks[index] = ordered(out, swap) if swap_mask else out
            else:
                for_first, for_second = local_factors(pair_w, swap, shift)
                for index, pair in enumerate(chunks):
                    out = dot(for_first, pair[0], level) + dot(for_second, pair[1], level)
                    chunks[index] = [out[:rank], out[rank:]]
            if last:
                sorted_for = swap_mask
    assert sorted_for == place.mask
    flag = jnp.zeros((1,), jnp.int32)
    result = None
    for start, pair in zip(starts, chunks):
        result = expand(flag, jnp.swapaxes(expander, 1, 2), pair, start, total, result)
    return result


def solution(mesh):
    placed = (
        P(None, AXES, None, None),
        P(None, AXES, None, None),
        P(None, None, AXES, None, None, None),
        P(AXES, None, None),
    )
    return jax.shard_map(
        shards, mesh=mesh, in_specs=placed, out_specs=P(AXES, None, None), check_vma=False
    )
```
